32 devices in a mesh: wide: 8 (over z, y), narrow: 4 (over x, core).
Axes of the slice: x: 2, y: 2, z: 4, core: 2. Of those that a mesh axis runs over, the one named last changes fastest.
Arguments:
- residual: float32 [8, 4, 6, 192, 512], P('wide', 'narrow'), may hold values from -6 to 6
- face_schur: float32 [8, 4, 6, 192, 192], P('wide', 'narrow'), may hold values from -0.5 to 1.5, as said below
- local_solver: bfloat16 [8, 4, 1152, 1152], P('wide', 'narrow'), may hold values from -0.1875 to 0.1875
- interface_functional_set: float32 [3, 192, 16], replicated, may hold values from -0.4375 to 0.4375
- coarse_inverse: float32 [1536, 1536], P('wide', 'narrow'), may hold values from -0.3125 to 0.3125
Outputs:
- preconditioned: float32 [8, 4, 3, 192, 512], P('wide', 'narrow')
The draws below stay inside these ranges and needn't reach their ends.
Inputs may be any that keep to these rules, and one draw needn't show every extreme that they name: `face_schur`: every face block is symmetric positive definite.
All inputs are finite; a program needn't handle non-finite values. Where the reference program divides by a largest or mean magnitude, that divisor is 1e-20 or more.
Results may differ from the reference program's by a relative error of at most 0.002.
Values sent between devices are 32-bit elements; how exact they have to be, the bound alone decides.
No kernel may reach another device: no remote copies, remote signals or barrier semaphores. Data moves between devices by JAX's collectives and lax.ppermute only.
A program may use at most 64 MiB of HBM per device.

```python
import jax
import jax.numpy as jnp
from jax import lax

F = 192
CF = 16
R = 512
NS_STEPS = 12
LOC = 1152
SUB_ROWS = 8
SUB_COLS = 4
NC = 1536


def draw_face_schur(key, part):
    scale_key, random_seed_blend = jax.random.split(jax.random.fold_in(key, 17))
    leading = (SUB_ROWS, SUB_COLS, 6)
    lowest = jnp.log(0.05)
    mixing = jax.random.normal(random_seed_blend, leading + (F, F), jnp.float32)
    stiffness = jnp.exp(jax.random.uniform(scale_key, leading + (F,), jnp.float32, 0.0, 1.0) * (0.0 - lowest) + lowest)
    mixing = (mixing + jnp.swapaxes(mixing, -1, -2)) * (0.2 / jnp.sqrt(2.0 * F))
    rooted = jnp.sqrt(stiffness)
    identity = jnp.eye(F, dtype=jnp.float32)
    return rooted[..., :, None] * (identity + mixing) * rooted[..., None, :]


def steps_of(own_key, extent, shards, least, top_value):
    factor_of, own = 1.0, jax.random.fold_in(own_key, 6)
    for position, parts in shards:
        steps = jnp.exp(jax.random.uniform(jax.random.fold_in(own, position), (parts,), jnp.float32, least / len(shards), top_value / len(shards)))
        factor_of = factor_of * jnp.repeat(steps, extent[position] // parts).reshape([-1 if axis == position else 1 for axis in range(len(extent))])
    return factor_of


def noise(own_key, dims, scale, bound, cuts=(), held_as=jnp.bfloat16):
    level = steps_of(own_key, dims, cuts, -0.22, 0.18) if cuts else 1.0
    drawn = jax.random.normal(own_key, dims, jnp.float32) * scale * level
    return jnp.minimum(jnp.maximum(drawn, -bound), bound).astype(held_as)


def setup_inputs(seed: int = 0) -> dict:
    keys = jax.random.split(jax.random.key(seed), 6)
    return {
        "residual": noise(keys[0], (SUB_ROWS, SUB_COLS, 6, F, R), 1.0, 6.0, ((0, 8), (1, 4)), jnp.float32),
        "face_schur": draw_face_schur(jax.random.fold_in(keys[5], 71), 0),
        "local_solver": noise(keys[2], (SUB_ROWS, SUB_COLS, LOC, LOC), LOC ** -0.5, 0.1875, ((0, 8), (1, 4))),
        "interface_functional_set": noise(keys[3], (3, F, CF), F ** -0.5, 0.4375, (), jnp.float32),
        "coarse_inverse": noise(keys[4], (NC, NC), (NC // 4) ** -0.5, 0.3125, ((0, 8), (1, 4)), jnp.float32),
    }


exact_arithmetic_mode = lax.Precision.HIGHEST


def newton_schulz(matrices):
    row_sums = jnp.max(jnp.sum(jnp.abs(matrices), axis=2), axis=1)
    approx = matrices / (row_sums * row_sums)[:, None, None]
    for iteration in range(NS_STEPS):
        product = jnp.einsum("bij,bjk->bik", matrices, approx, precision=exact_arithmetic_mode)
        approx = 2.0 * approx - jnp.einsum("bij,bjk->bik", approx, product, precision=exact_arithmetic_mode)
    return approx


def reference(residual, face_schur, local_solver, interface_functional_set, coarse_inverse):
    rows_count = residual.shape[0]
    cols_count = residual.shape[1]
    upper_wide = face_schur[:, :, 1] + jnp.roll(face_schur[:, :, 0], -1, axis=0)
    upper_narrow = face_schur[:, :, 3] + jnp.roll(face_schur[:, :, 2], -1, axis=1)
    vertical = face_schur[:, :, 4] + face_schur[:, :, 5]
    face_sums = jnp.stack([upper_wide, upper_narrow, vertical], axis=2)
    inverse = newton_schulz(face_sums.reshape(-1, F, F)).reshape(face_sums.shape)
    load_wide = residual[:, :, 1] + jnp.roll(residual[:, :, 0], -1, axis=0)
    load_narrow = residual[:, :, 3] + jnp.roll(residual[:, :, 2], -1, axis=1)
    load_vertical = residual[:, :, 4] + residual[:, :, 5]
    assembled_vector = jnp.stack([load_wide, load_narrow, load_vertical], axis=2)
    scaled = jnp.einsum("wngij,wngjr->wngir", inverse, assembled_vector, precision=exact_arithmetic_mode)
    face_scaled = jnp.stack([jnp.roll(scaled[:, :, 0], 1, axis=0), scaled[:, :, 0],
                             jnp.roll(scaled[:, :, 1], 1, axis=1), scaled[:, :, 1],
                             scaled[:, :, 2], scaled[:, :, 2]], axis=2)
    local_loads = jnp.einsum("wnfij,wnfjr->wnfir", face_schur, face_scaled, precision=exact_arithmetic_mode).astype(jnp.bfloat16)
    flattened = local_loads.reshape(-1, LOC, R)
    solvers = local_solver.reshape(-1, LOC, LOC)

    def solve_one(pair):
        return jnp.dot(pair[0], pair[1], preferred_element_type=jnp.float32)

    solved = lax.map(solve_one, (solvers, flattened)).reshape(rows_count, cols_count, 6, F, R)
    weighted = jnp.einsum("wnfij,wnfjr->wnfir", face_schur, solved, precision=exact_arithmetic_mode)
    combined = jnp.stack([weighted[:, :, 1] + jnp.roll(weighted[:, :, 0], -1, axis=0),
                          weighted[:, :, 3] + jnp.roll(weighted[:, :, 2], -1, axis=1),
                          weighted[:, :, 4] + weighted[:, :, 5]], axis=2)
    local_part = jnp.einsum("wngij,wngjr->wngir", inverse, combined, precision=exact_arithmetic_mode)
    restricted_residual = jnp.einsum("ehd,maeht->maedt", interface_functional_set, assembled_vector, precision=exact_arithmetic_mode)
    column_order = jnp.transpose(restricted_residual, (1, 0, 2, 3, 4)).reshape(NC, R)
    coarse_space = jnp.dot(coarse_inverse, column_order, precision=exact_arithmetic_mode, preferred_element_type=jnp.float32)
    coarse_space = coarse_space.reshape(rows_count, cols_count, 3, CF, R)
    coarse_component = jnp.einsum("luo,vqlos->vqlus", interface_functional_set, coarse_space, precision=exact_arithmetic_mode)
    return local_part + coarse_component
```

```python
import functools

import jax
import jax.numpy as jnp
from jax import lax
from jax.experimental import pallas as pl
from jax.experimental.pallas import tpu as pltpu
from jax.sharding import PartitionSpec as P

NS_STEPS = 12
LANES = 128
VMEM_BYTES = 24 * 2**20
F32 = jnp.float32
BF16 = jnp.bfloat16


def halves(value):
    high = value.astype(BF16)
    return high, (value - high.astype(F32)).astype(BF16)


def mxu(left, right):
    return jnp.dot(left, right, preferred_element_type=F32)


def product(left, right):
    left_high, left_low = left
    right_high, right_low = right
    return mxu(left_high, right_high) + (
        mxu(left_high, right_low) + mxu(left_low, right_high)
    )


def call(body, outs, args, flops=0, scratch=(), scalars=(), name=None):
    args = [*scalars, *args]
    count = len(scalars)
    touched = sum(a.size * a.dtype.itemsize for a in args)
    touched += sum(a.size * a.dtype.itemsize for a in outs)
    specs = [pl.BlockSpec(memory_space=pltpu.SMEM)] * count
    specs += [pl.BlockSpec(memory_space=pltpu.VMEM)] * (len(args) - count)
    return pl.pallas_call(
        body,
        out_shape=outs,
        in_specs=specs,
        out_specs=[pl.BlockSpec(memory_space=pltpu.VMEM)] * len(outs),
        scratch_shapes=list(scratch),
        cost_estimate=pl.CostEstimate(
            flops=flops, bytes_accessed=touched, transcendentals=0
        ),
        compiler_params=pltpu.CompilerParams(vmem_limit_bytes=VMEM_BYTES),
        name=name,
    )(*args)


def shape(*dims, dtype=F32):
    return jax.ShapeDtypeStruct(dims, dtype)


def packed_rows(order):
    return order + (order - LANES) // 2


def pack_block(block, out):
    order = block.shape[0]
    tail = order - LANES
    out[0:order, :] = block[:, 0:LANES]
    corner = block[LANES:, LANES:]
    out[order : order + tail // 2, :] = jnp.concatenate(
        [corner[: tail // 2], corner[tail // 2 :]], axis=1
    )


def add_packed(block, packed, out):
    order = block.shape[0]
    tail = order - LANES
    out[:, 0:LANES] = block[:, 0:LANES] + packed[0:order, :]
    out[0:LANES, LANES:] = block[0:LANES, LANES:] + packed[LANES:order, :].T
    corner = packed[order : order + tail // 2, :]
    out[LANES:, LANES:] = block[LANES:, LANES:] + jnp.concatenate(
        [corner[:, :tail], corner[:, tail:]], axis=0
    )


def pack_body(order, blocks, loads, functionals, wide_out, narrow_out, own_out):
    base = packed_rows(order)
    count = functionals.shape[2]
    columns = loads.shape[2]
    for face, kind, out in ((0, 0, wide_out), (2, 1, narrow_out)):
        pack_block(blocks[face], out)
        part = product(halves(functionals[kind].T), halves(loads[face]))
        for step in range(columns // LANES):
            out[base + step * count : base + (step + 1) * count, :] = part[
                :, step * LANES : (step + 1) * LANES
            ]
    for kind, value in enumerate((loads[1], loads[3], loads[4] + loads[5])):
        own_out[kind * count : (kind + 1) * count, :] = product(
            halves(functionals[kind].T), halves(value)
        )


def restricted_body(order, count, wide_in, narrow_in, own, out):
    base = packed_rows(order)
    columns = own.shape[1]
    for kind, packed in ((0, wide_in), (1, narrow_in)):
        for step in range(columns // LANES):
            lanes = slice(step * LANES, (step + 1) * LANES)
            out[kind * count : (kind + 1) * count, lanes] = (
                own[kind * count : (kind + 1) * count, lanes]
                + packed[base + step * count : base + (step + 1) * count, :]
            )
    out[2 * count :, :] = own[2 * count :, :]


def inverse_body(blocks, wide_in, narrow_in, high_out, low_out, sums, image, approx):
    add_packed(blocks[1], wide_in, sums.at[0])
    add_packed(blocks[3], narrow_in, sums.at[1])
    sums[2] = blocks[4] + blocks[5]
    for face in range(3):
        matrix = sums[face]
        largest = jnp.max(
            jnp.sum(jnp.abs(matrix), axis=1, keepdims=True), axis=0, keepdims=True
        )
        start = matrix / (largest * largest)
        approx[face] = start
        image[face] = product(halves(matrix), halves(start))
    for step in range(NS_STEPS):
        for face in range(3):
            current = image[face]
            left = halves(current)
            before = approx[face]
            after = 2.0 * before - product(left, halves(before))
            if step < NS_STEPS - 1:
                image[face] = 2.0 * current - product(left, left)
                approx[face] = after
            else:
                high_out[face], low_out[face] = halves(after)


def scaled_body(loads, wide_in, narrow_in, high, low, wide_out, narrow_out, own_out):
    for face, value, out in (
        (0, loads[1] + wide_in[...], wide_out),
        (1, loads[3] + narrow_in[...], narrow_out),
        (2, loads[4] + loads[5], own_out),
    ):
        out[...] = product((high[face], low[face]), halves(value))


def outgoing_body(
    blocks, solver, wide_below, wide_own, narrow_below, narrow_own, vertical,
    loads_out, wide_out, narrow_out,
):
    order = blocks.shape[1]
    for face, value in enumerate(
        (wide_below, wide_own, narrow_below, narrow_own, vertical, vertical)
    ):
        loads_out[face * order : (face + 1) * order, :] = product(
            halves(blocks[face]), halves(value[...])
        ).astype(BF16)
    for face, out in ((0, wide_out), (2, narrow_out)):
        solved = mxu(solver[face * order : (face + 1) * order, :], loads_out[...])
        out[...] = product(halves(blocks[face]), halves(solved))


def kept_body(blocks, solver, loads, out):
    order = blocks.shape[1]

    def weighted(face):
        solved = mxu(solver[face * order : (face + 1) * order, :], loads[...])
        return product(halves(blocks[face]), halves(solved))

    out[0] = weighted(1)
    out[1] = weighted(3)
    out[2] = weighted(4) + weighted(5)


def coarse_body(groups, index, matrix, pair, *rest):
    outs = rest[2 * (groups - 1) :]
    (*outs, gathered) = outs
    up, down = rest[: groups - 1], rest[groups - 1 : 2 * (groups - 1)]
    rows = pair.shape[0]
    place, across, members = index[0], index[1], len(outs)
    own = pl.multiple_of(place * rows, rows)
    gathered[pl.ds(own, rows), :] = pair[...]
    for step in range(1, groups):
        spot = lax.rem(place + step, groups)
        spot = pl.multiple_of(spot * rows, rows)
        gathered[pl.ds(spot, rows), :] = down[step - 1][...] + up[groups - 1 - step][...]
    total = product(halves(matrix[...]), halves(gathered[...]))
    gathered[0 : total.shape[0], :] = total
    share = outs[0].shape[0]
    for step in range(members):
        spot = pl.multiple_of(lax.rem(across + step, members) * share, share)
        outs[step][...] = gathered[pl.ds(spot, share), :]


def final_body(count, kept, high, low, wide_in, narrow_in, functionals, *rest):
    (*parts, out) = rest
    coarse = parts[0][...]
    for part in parts[1:]:
        coarse = coarse + part[...]
    for face in range(3):
        value = kept[face]
        if face == 0:
            value = value + wide_in[...]
        if face == 1:
            value = value + narrow_in[...]
        fine = product((high[face], low[face]), halves(value))
        rows = coarse[face * count : (face + 1) * count, :]
        out[face] = fine + product(halves(functionals[face]), halves(rows))


def passed_along(value, axis, steps):
    count = lax.axis_size(axis)
    pairs = [(source, (source + steps) % count) for source in range(count)]
    return lax.ppermute(value, axis, pairs)


def per_device(residual, face_schur, local_solver, functionals, coarse_inverse):
    blocks, loads, solver = face_schur[0, 0], residual[0, 0], local_solver[0, 0]
    order, columns = loads.shape[1:]
    count = functionals.shape[2]
    wide, narrow = lax.axis_size("wide"), lax.axis_size("narrow")
    field = shape(order, columns)
    field_flops = 6 * order * order * columns

    packed = shape(packed_rows(order) + count * columns // LANES, LANES)
    wide_low, narrow_low, own = call(
        functools.partial(pack_body, order),
        [packed, packed, shape(3 * count, columns)],
        [blocks, loads, functionals],
        flops=5 * 6 * order * columns * count,
        name="pack",
    )
    wide_above = passed_along(wide_low, "wide", -1)
    narrow_above = passed_along(narrow_low, "narrow", -1)
    wide_loads = passed_along(loads[0], "wide", -1)
    narrow_loads = passed_along(loads[2], "narrow", -1)

    (restricted,) = call(
        functools.partial(restricted_body, order, count),
        [shape(3 * count, columns)],
        [wide_above, narrow_above, own],
        name="restricted",
    )
    halved = shape(3, order, order, dtype=BF16)
    high, low = call(
        inverse_body,
        [halved, halved],
        [blocks, wide_above, narrow_above],
        flops=3 * 24 * 6 * order**3,
        scratch=[pltpu.VMEM((3, order, order), F32)] * 3,
        name="inverse",
    )

    pairing = 2 if wide % 2 == 0 else 1
    groups = wide // pairing
    if pairing == 2:
        other = lax.ppermute(restricted, "wide", [(i, i ^ 1) for i in range(wide)])
        first = lax.axis_index("wide") % 2 == 0
        pair = jnp.concatenate(
            [jnp.where(first, restricted, other), jnp.where(first, other, restricted)],
            axis=0,
        )
    else:
        pair = restricted
    up, down = [], []
    rising = falling = pair
    for step in range(1, groups):
        rising = lax.ppermute(
            rising,
            "wide",
            [
                (g * pairing + k, (g + 1) * pairing + k)
                for g in range(step - 1, groups - 1)
                for k in range(pairing)
            ],
        )
        falling = lax.ppermute(
            falling,
            "wide",
            [
                (g * pairing + k, (g - 1) * pairing + k)
                for g in range(1, groups - step + 1)
                for k in range(pairing)
            ],
        )
        up.append(rising)
        down.append(falling)
    place = jnp.stack([lax.axis_index("wide") // pairing, lax.axis_index("narrow")])
    share = shape(coarse_inverse.shape[0] // narrow, columns)
    shares = call(
        functools.partial(coarse_body, groups),
        [share] * narrow,
        [coarse_inverse, pair, *up, *down],
        flops=6 * coarse_inverse.size * columns,
        scratch=[pltpu.VMEM((max(coarse_inverse.shape), columns), F32)],
        scalars=[place.astype(jnp.int32)],
        name="coarse",
    )
    parts = [shares[0]]
    parts += [passed_along(shares[step], "narrow", step) for step in range(1, narrow)]

    wide_scaled, narrow_scaled, vertical = call(
        scaled_body,
        [field] * 3,
        [loads, wide_loads, narrow_loads, high, low],
        flops=3 * field_flops,
        name="scaled",
    )
    wide_below = passed_along(wide_scaled, "wide", 1)
    narrow_below = passed_along(narrow_scaled, "narrow", 1)
    local_loads, wide_back, narrow_back = call(
        outgoing_body,
        [shape(6 * order, columns, dtype=BF16), field, field],
        [blocks, solver, wide_below, wide_scaled, narrow_below, narrow_scaled, vertical],
        flops=8 * field_flops + 2 * 2 * 6 * order * order * columns,
        name="outgoing",
    )
    wide_returned = passed_along(wide_back, "wide", -1)
    narrow_returned = passed_along(narrow_back, "narrow", -1)
    (kept,) = call(
        kept_body,
        [shape(3, order, columns)],
        [blocks, solver, local_loads],
        flops=4 * field_flops + 4 * 2 * 6 * order * order * columns,
        name="kept",
    )
    (out,) = call(
        functools.partial(final_body, count),
        [shape(3, order, columns)],
        [kept, high, low, wide_returned, narrow_returned, functionals, *parts],
        flops=3 * field_flops,
        name="final",
    )
    return out[None, None]


def solution(mesh):
    placed = (
        P("wide", "narrow", None, None, None),
        P("wide", "narrow", None, None, None),
        P("wide", "narrow", None, None),
        P(),
        P("wide", "narrow"),
    )
    return jax.shard_map(
        per_device,
        mesh=mesh,
        in_specs=placed,
        out_specs=P("wide", "narrow", None, None, None),
        check_vma=False,
    )
```

```python
import functools

import jax
import jax.numpy as jnp
from jax import lax
from jax.experimental import pallas as pl
from jax.experimental.pallas import tpu as pltpu
from jax.sharding import PartitionSpec as P

NS_STEPS = 12
LANES = 128
VMEM_BYTES = 24 * 2**20
CUTS = 1
F32 = jnp.float32
BF16 = jnp.bfloat16


def halves(value):
    high = value.astype(BF16)
    return high, (value - high.astype(F32)).astype(BF16)


def mxu(left, right):
    return jnp.dot(left, right, preferred_element_type=F32)


def product(left, right):
    left_high, left_low = left
    right_high, right_low = right
    return mxu(left_high, right_high) + (
        mxu(left_high, right_low) + mxu(left_low, right_high)
    )


def call(
    body, outs, args, flops=0, scratch=(), apart=0, alias=None, far=False,
    vmem=VMEM_BYTES,
):
    touched = sum(a.size * a.dtype.itemsize for a in args)
    touched += sum(a.size * a.dtype.itemsize for a in outs)
    specs = [pl.BlockSpec(memory_space=pltpu.HBM)] * apart
    specs += [pl.BlockSpec(memory_space=pltpu.VMEM)] * (len(args) - apart)
    return pl.pallas_call(
        body,
        out_shape=outs,
        in_specs=specs,
        out_specs=[pl.BlockSpec(memory_space=pltpu.HBM if far else pltpu.VMEM)] * len(outs),
        input_output_aliases=alias or {},
        scratch_shapes=list(scratch),
        cost_estimate=pl.CostEstimate(
            flops=flops, bytes_accessed=touched, transcendentals=0
        ),
        compiler_params=pltpu.CompilerParams(vmem_limit_bytes=vmem),
    )(*args)


def shape(*dims, dtype=F32):
    return jax.ShapeDtypeStruct(dims, dtype)


def packed_rows(order):
    return order + (order - LANES) // 2


def pack_block(block, out):
    order = block.shape[0]
    tail = order - LANES
    out[0:order, :] = block[:, 0:LANES]
    corner = block[LANES:, LANES:]
    out[order : order + tail // 2, :] = jnp.concatenate(
        [corner[: tail // 2], corner[tail // 2 :]], axis=1
    )


def add_packed(block, packed, out):
    order = block.shape[0]
    tail = order - LANES
    out[:, 0:LANES] = block[:, 0:LANES] + packed[0:order, :]
    out[0:LANES, LANES:] = block[0:LANES, LANES:] + packed[LANES:order, :].T
    corner = packed[order : order + tail // 2, :]
    out[LANES:, LANES:] = block[LANES:, LANES:] + jnp.concatenate(
        [corner[:, :tail], corner[:, tail:]], axis=0
    )


def transposed(left, right):
    return lax.dot_general(
        left, right, (((0,), (0,)), ((), ())), preferred_element_type=F32
    )


def transposed(left, right):
    return lax.dot_general(
        left, right, (((0,), (0,)), ((), ())), preferred_element_type=F32
    )


def pack_body(blocks, loads, functionals, wide_out, narrow_out, narrow_loads, *rest):
    (*wide_loads, faces, first, ends, sems) = rest
    order = blocks.shape[1]
    base = packed_rows(order)
    count = functionals.shape[1]
    width = wide_loads[0].shape[1]
    copies = [
        pltpu.make_async_copy(blocks.at[0], faces.at[0], sems.at[0]),
        pltpu.make_async_copy(blocks.at[2], faces.at[1], sems.at[1]),
        pltpu.make_async_copy(loads.at[2], narrow_loads, sems.at[2]),
        pltpu.make_async_copy(loads.at[0], first, sems.at[3]),
        pltpu.make_async_copy(functionals.at[1], ends, sems.at[4]),
    ]
    for copy in copies:
        copy.start()
    copies[0].wait()
    pack_block(faces.at[0], wide_out)
    copies[1].wait()
    pack_block(faces.at[1], narrow_out)
    copies[4].wait()
    copies[2].wait()
    part = product(halves(ends[...]), halves(narrow_loads[...]))
    for step in range(part.shape[1] // LANES):
        narrow_out[base + step * count : base + (step + 1) * count, :] = part[
            :, step * LANES : (step + 1) * LANES
        ]
    copies[3].wait()
    for step, out in enumerate(wide_loads):
        out[...] = first[:, step * width : (step + 1) * width]


def own_body(order, narrow_in, loads, functionals, out):
    base = packed_rows(order)
    count = functionals.shape[1]
    for spot, kind, value in (
        (0, 0, loads[1]), (1, 1, loads[3]), (2, 2, loads[4] + loads[5]), (3, 0, loads[0])
    ):
        out[spot * count : (spot + 1) * count, :] = product(
            halves(functionals[kind]), halves(value)
        )
    for step in range(loads.shape[2] // LANES):
        lanes = slice(step * LANES, (step + 1) * LANES)
        part = narrow_in[base + step * count : base + (step + 1) * count, :]
        out[count : 2 * count, lanes] = out[count : 2 * count, lanes] + part


def pair_body(own, other, out):
    count = own.shape[0] // 4
    rows = 3 * count
    member = lax.rem(lax.axis_index("wide"), 2)
    out[pl.ds(pl.multiple_of(member * rows, 8), rows), :] = own[:rows]
    out[pl.ds(pl.multiple_of((1 - member) * rows, 8), rows), :] = other[:rows]
    mine, theirs = own[rows:], other[rows:]
    out[0:count, :] = out[0:count, :] + jnp.where(member == 0, theirs, mine)
    out[2 * rows :, :] = jnp.where(member == 0, mine, theirs)


def inverse_body(blocks, wide_in, narrow_in, high_out, low_out, sums, image, approx):
    add_packed(blocks[1], wide_in, sums.at[0])
    add_packed(blocks[3], narrow_in, sums.at[1])
    sums[2] = blocks[4] + blocks[5]
    for face in range(3):
        matrix = sums[face]
        largest = jnp.max(
            jnp.sum(jnp.abs(matrix), axis=1, keepdims=True), axis=0, keepdims=True
        )
        start = matrix / (largest * largest)
        approx[face] = start
        image[face] = product(halves(matrix), halves(start))
    for step in range(NS_STEPS):
        for face in range(3):
            current = image[face]
            left = halves(current)
            before = approx[face]
            after = 2.0 * before - product(left, halves(before))
            if step < NS_STEPS - 1:
                image[face] = 2.0 * current - product(left, left)
                approx[face] = after
            else:
                high_out[face], low_out[face] = halves(after)


def scaled_body(cut, loads, wide_in, narrow_in, high, low, wide_out, narrow_out, own_out):
    width = wide_in.shape[1]
    columns = slice(cut * width, (cut + 1) * width)
    for face, value, out in (
        (0, loads[1, :, columns] + wide_in[...], wide_out),
        (1, loads[3, :, columns] + narrow_in[:, columns], narrow_out),
        (2, loads[4, :, columns] + loads[5, :, columns], own_out),
    ):
        out[...] = product((high[face], low[face]), halves(value))


def outgoing_body(
    blocks, solver, wide_below, wide_own, narrow_below, narrow_own, vertical,
    loads_out, wide_out, narrow_out,
):
    order = blocks.shape[1]
    for face, value in enumerate(
        (wide_below, wide_own, narrow_below, narrow_own, vertical, vertical)
    ):
        loads_out[face * order : (face + 1) * order, :] = product(
            halves(blocks[face]), halves(value[...])
        ).astype(BF16)
    for face, out in ((0, wide_out), (2, narrow_out)):
        solved = mxu(solver[face * order : (face + 1) * order, :], loads_out[...])
        out[...] = product(halves(blocks[face]), halves(solved))


def kept_body(blocks, solver, high, low, *rest):
    (*loads, out, solved) = rest
    order = blocks.shape[1]
    width = loads[0].shape[1]
    for cut in range(CUTS):
        columns = slice(cut * width, (cut + 1) * width)
        solved[0:order] = mxu(solver[order : 2 * order, :], loads[cut][...])
        solved[order:] = mxu(solver[3 * order :, :], loads[cut][...])

        def weighted(face, spot):
            return product(
                halves(blocks[face]), halves(solved[spot * order : (spot + 1) * order])
            )

        for face, value in (
            (0, weighted(1, 0)), (1, weighted(3, 1)), (2, weighted(4, 2) + weighted(5, 3))
        ):
            out[face, :, columns] = product((high[face], low[face]), halves(value))


def returned_body(kept, high, low, *rest):
    (*fields, wide_out, narrow_out) = rest
    for cut in range(CUTS):
        width = fields[2 * cut].shape[1]
        columns = slice(cut * width, (cut + 1) * width)
        for face, out in ((0, wide_out), (1, narrow_out)):
            out[:, columns] = kept[face, :, columns] + product(
                (high[face], low[face]), halves(fields[2 * cut + face][...])
            )


def ring_origin(groups, step):
    group = lax.div(lax.axis_index("wide"), lax.axis_size("wide") // groups)
    origin = jnp.int32(0)
    for own in range(groups):
        other = ring_group(ring_place(own, groups) + step, groups)
        origin = jnp.where(group == own, other, origin)
    return origin


def hand_out(total, outs):
    across, members = lax.axis_index("narrow"), len(outs)
    share = outs[0].shape[0]
    for step in range(members):
        spot = pl.multiple_of(lax.rem(across + step, members) * share, 8)
        outs[step][...] = total[pl.ds(spot, share), :]


def lent_body(pairing, groups, matrix, out):
    count = out.shape[1] // (3 * pairing + 1)
    rows = 3 * count
    origin = ring_origin(groups, groups // 2)
    for group in range(groups):

        @pl.when(origin == group)
        def _(first=group * pairing):
            last = (first - 1) % (pairing * groups)
            out[...] = jnp.concatenate(
                [
                    matrix[:, first * rows : (first + pairing) * rows],
                    matrix[:, last * rows : last * rows + count],
                ],
                axis=1,
            )


def far_body(held, pair, *rest):
    (*outs, total) = rest
    total[...] = product(halves(held[...]), halves(pair[...]))
    hand_out(total, outs)


def sum_body(*rest):
    (*parts, out) = rest
    total = parts[0][...]
    for part in parts[1:]:
        total = total + part[...]
    out[...] = total


def coarse_body(pairing, groups, matrix, *rest):
    steps = [step for step in range(groups) if 2 * step != groups]
    received = 1 + (len(steps) - 1) * pairing
    copies, (*outs, gathered) = rest[:received], rest[received:]
    member = lax.rem(lax.axis_index("wide"), pairing)
    chunks = [copies[0]]
    for first in range(1, received, pairing):
        chunk = copies[first][...]
        for other in range(1, pairing):
            chunk = jnp.where(member == other, copies[first + other][...], chunk)
        chunks.append(chunk)
    count = chunks[0].shape[0] // (3 * pairing + 1)
    rows = 3 * count
    spots = [ring_origin(groups, step) * pairing for step in steps]
    if len(steps) < groups:
        spot = pl.multiple_of(ring_origin(groups, groups // 2) * pairing * rows, 8)
        gathered[pl.ds(spot, pairing * rows), :] = jnp.zeros(
            (pairing * rows, gathered.shape[1]), F32
        )
    for spot, chunk in zip(spots, chunks):
        spot = pl.multiple_of(spot * rows, 8)
        gathered[pl.ds(spot, pairing * rows), :] = chunk[: pairing * rows]
    for spot, chunk in zip(spots, chunks):
        spot = lax.rem(spot + pairing * groups - 1, pairing * groups)
        spot = pl.ds(pl.multiple_of(spot * rows, 8), count)
        gathered[spot, :] = gathered[spot, :] + chunk[pairing * rows :]
    total = product(halves(matrix[...]), halves(gathered[0 : matrix.shape[1]]))
    gathered[0 : total.shape[0], :] = total
    hand_out(gathered, outs)


def final_body(kept, wide_part, narrow_part, functionals, *rest):
    (*parts, out, held, sems) = rest
    count = functionals.shape[1]
    coarse = parts[0][...]
    for part in parts[1:]:
        coarse = coarse + part[...]
    copies = []
    for face, local in enumerate((wide_part[...], narrow_part[...], kept[2])):
        rows_high, rows_low = halves(coarse[face * count : (face + 1) * count])
        ends_high, ends_low = halves(functionals[face])
        held[face] = local + (
            transposed(ends_high, rows_high)
            + (transposed(ends_high, rows_low) + transposed(ends_low, rows_high))
        )
        copies.append(pltpu.make_async_copy(held.at[face], out.at[face], sems.at[face]))
        copies[-1].start()
    for copy in copies:
        copy.wait()


def passed_along(value, axis, steps):
    count = lax.axis_size(axis)
    pairs = [(source, (source + steps) % count) for source in range(count)]
    return lax.ppermute(value, axis, pairs)


def ring_group(place, groups):
    place = place % groups
    if place == 0:
        return 0
    return 2 * place - 1 if place <= groups // 2 else 2 * (groups - place)


def ring_place(group, groups):
    return next(p for p in range(groups) if ring_group(p, groups) == group)


def round_ring(value, pairing, steps, only=None):
    groups = lax.axis_size("wide") // pairing
    pairs = [
        (
            ring_group(place, groups) * pairing + member,
            ring_group(place + steps * (only in (None, member)), groups) * pairing
            + member,
        )
        for place in range(groups)
        for member in range(pairing)
    ]
    return lax.ppermute(value, "wide", pairs)


def apply(residual, face_schur, local_solver, functionals, coarse_inverse):
    blocks, loads, solver = face_schur[0, 0], residual[0, 0], local_solver[0, 0]
    functionals = jnp.swapaxes(functionals, 1, 2)
    order, columns = loads.shape[1:]
    count = functionals.shape[1]
    wide, narrow = lax.axis_size("wide"), lax.axis_size("narrow")
    width = columns // CUTS
    field, strip = shape(order, columns), shape(order, width)
    strip_flops = 6 * order * order * width

    base = packed_rows(order)
    wide_low, narrow_low, narrow_first, *wide_first = call(
        pack_body,
        [shape(base, LANES), shape(base + count * columns // LANES, LANES), field]
        + [strip] * CUTS,
        [
            pltpu.with_memory_space_constraint(blocks, pltpu.HBM),
            pltpu.with_memory_space_constraint(loads, pltpu.HBM),
            pltpu.with_memory_space_constraint(functionals, pltpu.HBM),
        ],
        flops=6 * order * columns * count,
        scratch=[
            pltpu.VMEM((2, order, order), F32),
            pltpu.VMEM((order, columns), F32),
            pltpu.VMEM((count, order), F32),
            pltpu.SemaphoreType.DMA((5,)),
        ],
        apart=3,
        vmem=VMEM_BYTES,
    )
    wide_above = passed_along(wide_low, "wide", -1)
    narrow_above = passed_along(narrow_low, "narrow", -1)
    wide_loads = [passed_along(wide_first[0], "wide", -1)]
    narrow_loads = passed_along(narrow_first, "narrow", -1)
    (own,) = call(
        functools.partial(own_body, order),
        [shape(4 * count, columns)],
        [narrow_above, loads, functionals],
        flops=4 * 6 * order * columns * count,
    )

    pairing = 2 if wide % 2 == 0 else 1
    groups = wide // pairing
    pair = own
    if pairing == 2:
        other = lax.ppermute(own, "wide", [(i, i ^ 1) for i in range(wide)])
        (pair,) = call(pair_body, [shape(7 * count, columns)], [own, other])
    wide_loads += [passed_along(wide_first[cut], "wide", -1) for cut in range(1, CUTS)]
    chunks = {0: [pair]}
    for member in range(pairing):
        rising = falling = pair
        for step in range(1, (groups + 1) // 2):
            rising = round_ring(rising, pairing, 1, member)
            falling = round_ring(falling, pairing, -1, member)
            chunks.setdefault(groups - step, []).append(rising)
            chunks.setdefault(step, []).append(falling)
    share = shape(coarse_inverse.shape[0] // narrow, columns)
    parts = []
    if groups % 2 == 0:
        (lent,) = call(
            functools.partial(lent_body, pairing, groups),
            [shape(coarse_inverse.shape[0], pair.shape[0])],
            [coarse_inverse],
        )
        held = round_ring(lent, pairing, groups // 2)
        far = call(
            far_body,
            [share] * narrow,
            [held, pair],
            flops=6 * held.size * columns,
            scratch=[pltpu.VMEM((coarse_inverse.shape[0], columns), F32)],
        )
        (gone,) = call(
            sum_body,
            [share],
            [far[0]]
            + [passed_along(far[step], "narrow", step) for step in range(1, narrow)],
        )
        parts.append(round_ring(gone, pairing, groups // 2))

    halved = shape(3, order, order, dtype=BF16)
    high, low = call(
        inverse_body,
        [halved, halved],
        [blocks, wide_above, narrow_above],
        flops=3 * 24 * 6 * order**3,
        scratch=[pltpu.VMEM((3, order, order), F32)] * 3,
    )
    shares = call(
        functools.partial(coarse_body, pairing, groups),
        [share] * narrow,
        [coarse_inverse, *(part for step in sorted(chunks) for part in chunks[step])],
        flops=6 * coarse_inverse.size * columns,
        scratch=[pltpu.VMEM((max(coarse_inverse.shape), columns), F32)],
    )
    parts.append(shares[0])
    parts += [passed_along(shares[step], "narrow", step) for step in range(1, narrow)]

    fields = []
    for cut in range(CUTS):
        wide_scaled, narrow_scaled, vertical = call(
            functools.partial(scaled_body, cut),
            [strip] * 3,
            [loads, wide_loads[cut], narrow_loads, high, low],
            flops=3 * strip_flops,
        )
        wide_below = passed_along(wide_scaled, "wide", 1)
        narrow_below = passed_along(narrow_scaled, "narrow", 1)
        fields.append((wide_below, wide_scaled, narrow_below, narrow_scaled, vertical))
    local_loads, returned = [], []
    for cut in range(CUTS):
        strip_loads, wide_back, narrow_back = call(
            outgoing_body,
            [shape(6 * order, width, dtype=BF16), strip, strip],
            [blocks, solver, *fields[cut]],
            flops=8 * strip_flops + 2 * 2 * 6 * order * order * width,
        )
        local_loads.append(strip_loads)
        returned.append(
            (
                passed_along(wide_back, "wide", -1),
                passed_along(narrow_back, "narrow", -1),
            )
        )
    (kept,) = call(
        kept_body,
        [shape(3, order, columns)],
        [blocks, solver, high, low, *local_loads],
        flops=CUTS * (7 * strip_flops + 4 * 2 * 6 * order * order * width),
        scratch=[pltpu.VMEM((4 * order, width), F32)],
    )
    wide_part, narrow_part = call(
        returned_body,
        [field, field],
        [kept, high, low, *(part for both in returned for part in both)],
        flops=CUTS * 2 * strip_flops,
    )
    (out,) = call(
        final_body,
        [shape(3, order, columns)],
        [kept, wide_part, narrow_part, functionals, *parts],
        flops=3 * 6 * order * count * columns,
        scratch=[pltpu.VMEM((3, order, columns), F32), pltpu.SemaphoreType.DMA((3,))],
        far=True,
    )
    return out[None, None]


def solution(mesh):
    placed = (
        P("wide", "narrow", None, None, None),
        P("wide", "narrow", None, None, None),
        P("wide", "narrow", None, None),
        P(),
        P("wide", "narrow"),
    )
    return jax.shard_map(
        apply,
        mesh=mesh,
        in_specs=placed,
        out_specs=P("wide", "narrow", None, None, None),
        check_vma=False,
    )
```

```python
import functools

import jax
import jax.numpy as jnp
from jax import lax
from jax.experimental import pallas as pl
from jax.experimental.pallas import tpu as pltpu
from jax.sharding import PartitionSpec as P

NS_STEPS = 12
LANES = 128
VMEM_BYTES = 24 * 2**20
F32 = jnp.float32
BF16 = jnp.bfloat16


def halves(value):
    high = value.astype(BF16)
    return high, (value - high.astype(F32)).astype(BF16)


def mxu(left, right):
    return jnp.dot(left, right, preferred_element_type=F32)


def product(left, right):
    left_high, left_low = left
    right_high, right_low = right
    return mxu(left_high, right_high) + (
        mxu(left_high, right_low) + mxu(left_low, right_high)
    )


def call(body, outs, args, flops=0, scratch=(), apart=0, far=False):
    touched = sum(a.size * a.dtype.itemsize for a in args)
    touched += sum(a.size * a.dtype.itemsize for a in outs)
    specs = [pl.BlockSpec(memory_space=pltpu.HBM)] * apart
    specs += [pl.BlockSpec(memory_space=pltpu.VMEM)] * (len(args) - apart)
    return pl.pallas_call(
        body,
        out_shape=outs,
        in_specs=specs,
        out_specs=[pl.BlockSpec(memory_space=pltpu.HBM if far else pltpu.VMEM)] * len(outs),
        scratch_shapes=list(scratch),
        cost_estimate=pl.CostEstimate(
            flops=flops, bytes_accessed=touched, transcendentals=0
        ),
        compiler_params=pltpu.CompilerParams(vmem_limit_bytes=VMEM_BYTES),
    )(*args)


def shape(*dims, dtype=F32):
    return jax.ShapeDtypeStruct(dims, dtype)


def packed_rows(order):
    return order + (order - LANES) // 2


def pack_block(block, out):
    order = block.shape[0]
    tail = order - LANES
    out[0:order, :] = block[:, 0:LANES]
    corner = block[LANES:, LANES:]
    out[order : order + tail // 2, :] = jnp.concatenate(
        [corner[: tail // 2], corner[tail // 2 :]], axis=1
    )


def add_packed(block, packed, out):
    order = block.shape[0]
    tail = order - LANES
    out[:, 0:LANES] = block[:, 0:LANES] + packed[0:order, :]
    out[0:LANES, LANES:] = block[0:LANES, LANES:] + packed[LANES:order, :].T
    corner = packed[order : order + tail // 2, :]
    out[LANES:, LANES:] = block[LANES:, LANES:] + jnp.concatenate(
        [corner[:, :tail], corner[:, tail:]], axis=0
    )


def transposed(left, right):
    return lax.dot_general(
        left, right, (((0,), (0,)), ((), ())), preferred_element_type=F32
    )


def transposed(left, right):
    return lax.dot_general(
        left, right, (((0,), (0,)), ((), ())), preferred_element_type=F32
    )


def pack_body(
    blocks, loads, functionals, wide_out, narrow_out, wide_loads, narrow_loads,
    faces, ends, sems,
):
    order = blocks.shape[1]
    base = packed_rows(order)
    count = functionals.shape[1]
    work = ((0, 0, wide_out, wide_loads), (2, 1, narrow_out, narrow_loads))
    copies = [pltpu.make_async_copy(functionals, ends, sems.at[0])]
    for face, kind, _, field in work:
        copies += [
            pltpu.make_async_copy(blocks.at[face], faces.at[kind], sems.at[2 * kind + 1]),
            pltpu.make_async_copy(loads.at[face], field, sems.at[2 * kind + 2]),
        ]
    for copy in copies:
        copy.start()
    copies[0].wait()
    for face, kind, out, field in work:
        copies[2 * kind + 1].wait()
        pack_block(faces.at[kind], out)
        copies[2 * kind + 2].wait()
        part = product(halves(ends[kind]), halves(field[...]))
        for step in range(part.shape[1] // LANES):
            out[base + step * count : base + (step + 1) * count, :] = part[
                :, step * LANES : (step + 1) * LANES
            ]


def own_body(order, wide_in, narrow_in, loads, functionals, out):
    base = packed_rows(order)
    count = functionals.shape[1]
    for kind, value in enumerate((loads[1], loads[3], loads[4] + loads[5])):
        out[kind * count : (kind + 1) * count, :] = product(
            halves(functionals[kind]), halves(value)
        )
    for kind, packed in ((0, wide_in), (1, narrow_in)):
        rows = slice(kind * count, (kind + 1) * count)
        for step in range(loads.shape[2] // LANES):
            lanes = slice(step * LANES, (step + 1) * LANES)
            part = packed[base + step * count : base + (step + 1) * count, :]
            out[rows, lanes] = out[rows, lanes] + part


def pair_body(own, other, out):
    rows = own.shape[0]
    member = lax.rem(lax.axis_index("wide"), 2)
    out[pl.ds(pl.multiple_of(member * rows, 8), rows), :] = own[...]
    out[pl.ds(pl.multiple_of((1 - member) * rows, 8), rows), :] = other[...]


def inverse_body(blocks, wide_in, narrow_in, high_out, low_out, sums, image, approx):
    add_packed(blocks[1], wide_in, sums.at[0])
    add_packed(blocks[3], narrow_in, sums.at[1])
    sums[2] = blocks[4] + blocks[5]
    for face in range(3):
        matrix = sums[face]
        largest = jnp.max(
            jnp.sum(jnp.abs(matrix), axis=1, keepdims=True), axis=0, keepdims=True
        )
        start = matrix / (largest * largest)
        approx[face] = start
        image[face] = product(halves(matrix), halves(start))
    for step in range(NS_STEPS):
        for face in range(3):
            current = image[face]
            left = halves(current)
            before = approx[face]
            after = 2.0 * before - product(left, halves(before))
            if step < NS_STEPS - 1:
                image[face] = 2.0 * current - product(left, left)
                approx[face] = after
            else:
                high_out[face], low_out[face] = halves(after)


def scaled_body(loads, wide_in, narrow_in, high, low, wide_out, narrow_out, own_out):
    for face, value, out in (
        (0, loads[1] + wide_in[...], wide_out),
        (1, loads[3] + narrow_in[...], narrow_out),
        (2, loads[4] + loads[5], own_out),
    ):
        out[...] = product((high[face], low[face]), halves(value))


def outgoing_body(
    blocks, solver, wide_below, wide_own, narrow_below, narrow_own, vertical,
    loads_out, wide_out, narrow_out,
):
    order = blocks.shape[1]
    for face, value in enumerate(
        (wide_below, wide_own, narrow_below, narrow_own, vertical, vertical)
    ):
        loads_out[face * order : (face + 1) * order, :] = product(
            halves(blocks[face]), halves(value[...])
        ).astype(BF16)
    for face, out in ((0, wide_out), (2, narrow_out)):
        solved = mxu(solver[face * order : (face + 1) * order, :], loads_out[...])
        out[...] = product(halves(blocks[face]), halves(solved))


def kept_body(blocks, solver, high, low, loads, out, solved):
    order = blocks.shape[1]
    solved[0:order] = mxu(solver[order : 2 * order, :], loads[...])
    solved[order:] = mxu(solver[3 * order :, :], loads[...])

    def weighted(face, spot):
        return product(
            halves(blocks[face]), halves(solved[spot * order : (spot + 1) * order])
        )

    for face, value in (
        (0, weighted(1, 0)), (1, weighted(3, 1)), (2, weighted(4, 2) + weighted(5, 3))
    ):
        out[face] = product((high[face], low[face]), halves(value))


def returned_body(kept, high, low, wide_in, narrow_in, wide_out, narrow_out):
    for face, value, out in ((0, wide_in, wide_out), (1, narrow_in, narrow_out)):
        out[...] = kept[face] + product((high[face], low[face]), halves(value[...]))


def ring_group(place, groups):
    place = place % groups
    if place == 0:
        return 0
    return 2 * place - 1 if place <= groups // 2 else 2 * (groups - place)


def ring_place(group, groups):
    return next(p for p in range(groups) if ring_group(p, groups) == group)


def ring_origin(groups, step):
    group = lax.div(lax.axis_index("wide"), lax.axis_size("wide") // groups)
    origin = jnp.int32(0)
    for own in range(groups):
        other = ring_group(ring_place(own, groups) + step, groups)
        origin = jnp.where(group == own, other, origin)
    return origin


def lent_body(groups, matrix, out):
    width = out.shape[1]
    origin = ring_origin(groups, groups // 2)
    for group in range(groups):

        @pl.when(origin == group)
        def _():
            out[...] = matrix[:, group * width : (group + 1) * width]


def far_body(held, pair, kept, sent, total):
    total[...] = product(halves(held[...]), halves(pair[...]))
    across, members = lax.axis_index("narrow"), lax.axis_size("narrow")
    share = total.shape[0] // members
    for out, first in ((kept, 0), (sent, 1)):
        for place, step in enumerate(range(first, members, 2)):
            spot = pl.multiple_of((across ^ step) * share, 8)
            out[place * share : (place + 1) * share] = total[pl.ds(spot, share), :]


def fold_body(share, kept_in, received, kept, sent):
    for place in range(kept_in.shape[0] // share):
        span = slice(place * share, (place + 1) * share)
        out = (kept, sent)[place % 2]
        spot = place // 2 * share
        out[spot : spot + share] = kept_in[span] + received[span]


def sum_body(kept_in, received, out):
    out[...] = kept_in[...] + received[...]


def coarse_body(groups, matrix, *rest):
    steps = [step for step in range(1, groups) if 2 * step != groups]
    copies, (*outs, gathered) = rest[: 1 + 2 * len(steps)], rest[1 + 2 * len(steps) :]
    length = copies[0].shape[0]
    member = lax.rem(lax.axis_index("wide"), 2)

    def rows(step):
        spot = ring_origin(groups, step) * length
        return pl.ds(pl.multiple_of(spot, 8), length)

    gathered[rows(0), :] = copies[0][...]
    gathered[rows(groups // 2), :] = jnp.zeros_like(copies[0])
    for place, step in enumerate(steps):
        even, odd = copies[1 + 2 * place : 3 + 2 * place]
        gathered[rows(step), :] = jnp.where(member == 0, even[...], odd[...])
    total = product(halves(matrix[...]), halves(gathered[0 : matrix.shape[1]]))
    gathered[0 : total.shape[0], :] = total
    across, members = lax.axis_index("narrow"), len(outs)
    share = outs[0].shape[0]
    for step in range(members):
        spot = pl.multiple_of(lax.rem(across + step, members) * share, 8)
        outs[step][...] = gathered[pl.ds(spot, share), :]


def final_body(kept, wide_part, narrow_part, functionals, *rest):
    (*parts, out, held, sems) = rest
    count = functionals.shape[1]
    coarse = parts[0][...]
    for part in parts[1:]:
        coarse = coarse + part[...]
    copies = []
    for face, local in enumerate((wide_part[...], narrow_part[...], kept[2])):
        rows_high, rows_low = halves(coarse[face * count : (face + 1) * count])
        ends_high, ends_low = halves(functionals[face])
        held[face] = local + (
            transposed(ends_high, rows_high)
            + (transposed(ends_high, rows_low) + transposed(ends_low, rows_high))
        )
        copies.append(pltpu.make_async_copy(held.at[face], out.at[face], sems.at[face]))
        copies[-1].start()
    for copy in copies:
        copy.wait()


def along(value, axis, target):
    pairs = [(source, target(source)) for source in range(lax.axis_size(axis))]
    return lax.ppermute(value, axis, pairs)


def shifted(value, axis, steps):
    count = lax.axis_size(axis)
    return along(value, axis, lambda source: (source + steps) % count)


def apply(residual, face_schur, local_solver, functionals, coarse_inverse):
    blocks, loads, solver = face_schur[0, 0], residual[0, 0], local_solver[0, 0]
    functionals = jnp.swapaxes(functionals, 1, 2)
    order, columns = loads.shape[1:]
    count = functionals.shape[1]
    wide, narrow = lax.axis_size("wide"), lax.axis_size("narrow")
    field = shape(order, columns)
    field_flops = 6 * order * order * columns

    packed = shape(packed_rows(order) + count * columns // LANES, LANES)
    wide_low, narrow_low, wide_first, narrow_first = call(
        pack_body,
        [packed, packed, field, field],
        [
            pltpu.with_memory_space_constraint(blocks, pltpu.HBM),
            pltpu.with_memory_space_constraint(loads, pltpu.HBM),
            pltpu.with_memory_space_constraint(functionals, pltpu.HBM),
        ],
        flops=2 * 6 * order * columns * count,
        scratch=[
            pltpu.VMEM((2, order, order), F32),
            pltpu.VMEM(functionals.shape, F32),
            pltpu.SemaphoreType.DMA((5,)),
        ],
        apart=3,
    )
    wide_above = shifted(wide_low, "wide", -1)
    narrow_above = shifted(narrow_low, "narrow", -1)
    wide_loads = shifted(wide_first, "wide", -1)
    narrow_loads = shifted(narrow_first, "narrow", -1)
    (own,) = call(
        functools.partial(own_body, order),
        [shape(3 * count, columns)],
        [wide_above, narrow_above, loads, functionals],
        flops=3 * 6 * order * columns * count,
    )
    halved = shape(3, order, order, dtype=BF16)
    high, low = call(
        inverse_body,
        [halved, halved],
        [blocks, wide_above, narrow_above],
        flops=3 * 24 * 6 * order**3,
        scratch=[pltpu.VMEM((3, order, order), F32)] * 3,
    )

    groups = wide // 2
    assert wide % 4 == 0 and narrow & (narrow - 1) == 0 and narrow > 1
    other = along(own, "wide", lambda i: i ^ 1)
    (pair,) = call(pair_body, [shape(6 * count, columns)], [own, other])

    def round_ring(value, steps, members):
        def target(i):
            if i % 2 not in members:
                return i
            place = ring_place(i // 2, groups) + steps
            return 2 * ring_group(place, groups) + i % 2

        return along(value, "wide", target)

    chunks = {}
    for member in range(2):
        rising = falling = pair
        for step in range(1, groups // 2):
            rising = round_ring(rising, 1, (member,))
            falling = round_ring(falling, -1, (member,))
            chunks[groups - step, member] = rising
            chunks[step, member] = falling
    rows = coarse_inverse.shape[0]
    share = shape(rows // narrow, columns)
    (lent,) = call(
        functools.partial(lent_body, groups),
        [shape(rows, pair.shape[0])],
        [coarse_inverse],
    )
    held = round_ring(lent, groups // 2, (0, 1))
    staying, going = call(
        far_body,
        [shape(rows // 2, columns)] * 2,
        [held, pair],
        flops=6 * held.size * columns,
        scratch=[pltpu.VMEM((rows, columns), F32)],
    )
    step = 1
    while 2 * step < narrow:
        received = along(going, "narrow", lambda j: j ^ step)
        step = 2 * step
        staying, going = call(
            functools.partial(fold_body, rows // narrow),
            [shape(rows // (2 * step), columns)] * 2,
            [staying, received],
        )
    received = along(going, "narrow", lambda j: j ^ step)
    (gone,) = call(sum_body, [share], [staying, received])
    home_coarse = round_ring(gone, groups // 2, (0, 1))
    shares = call(
        functools.partial(coarse_body, groups),
        [share] * narrow,
        [coarse_inverse, pair] + [chunks[key] for key in sorted(chunks)],
        flops=6 * coarse_inverse.size * columns,
        scratch=[pltpu.VMEM((max(coarse_inverse.shape), columns), F32)],
    )
    parts = [home_coarse, shares[0]] + [
        shifted(shares[step], "narrow", step) for step in range(1, narrow)
    ]

    wide_scaled, narrow_scaled, vertical = call(
        scaled_body,
        [field] * 3,
        [loads, wide_loads, narrow_loads, high, low],
        flops=3 * field_flops,
    )
    wide_below = shifted(wide_scaled, "wide", 1)
    narrow_below = shifted(narrow_scaled, "narrow", 1)
    local_loads, wide_back, narrow_back = call(
        outgoing_body,
        [shape(6 * order, columns, dtype=BF16), field, field],
        [blocks, solver, wide_below, wide_scaled, narrow_below, narrow_scaled, vertical],
        flops=8 * field_flops + 2 * 2 * 6 * order * order * columns,
    )
    wide_returned = shifted(wide_back, "wide", -1)
    narrow_returned = shifted(narrow_back, "narrow", -1)
    (kept,) = call(
        kept_body,
        [shape(3, order, columns)],
        [blocks, solver, high, low, local_loads],
        flops=7 * field_flops + 4 * 2 * 6 * order * order * columns,
        scratch=[pltpu.VMEM((4 * order, columns), F32)],
    )
    wide_part, narrow_part = call(
        returned_body,
        [field, field],
        [kept, high, low, wide_returned, narrow_returned],
        flops=2 * field_flops,
    )
    (out,) = call(
        final_body,
        [shape(3, order, columns)],
        [kept, wide_part, narrow_part, functionals, *parts],
        flops=3 * 6 * order * count * columns,
        scratch=[pltpu.VMEM((3, order, columns), F32), pltpu.SemaphoreType.DMA((3,))],
        far=True,
    )
    return out[None, None]


def solution(mesh):
    placed = (
        P("wide", "narrow", None, None, None),
        P("wide", "narrow", None, None, None),
        P("wide", "narrow", None, None),
        P(),
        P("wide", "narrow"),
    )
    return jax.shard_map(
        apply,
        mesh=mesh,
        in_specs=placed,
        out_specs=P("wide", "narrow", None, None, None),
        check_vma=False,
    )
```

```python
import functools

import jax
import jax.numpy as jnp
from jax import lax
from jax.experimental import pallas as pl
from jax.experimental.pallas import tpu as pltpu
from jax.sharding import PartitionSpec as P

NS_STEPS = 12
LANES = 128
VMEM_BYTES = 24 * 2**20
F32 = jnp.float32
BF16 = jnp.bfloat16


def halves(value):
    high = value.astype(BF16)
    return high, (value - high.astype(F32)).astype(BF16)


def mxu(left, right):
    return jnp.dot(left, right, preferred_element_type=F32)


def product(left, right):
    left_high, left_low = left
    right_high, right_low = right
    return mxu(left_high, right_high) + (
        mxu(left_high, right_low) + mxu(left_low, right_high)
    )


def call(body, outs, args, flops=0, scratch=(), apart=0, far=False):
    touched = sum(a.size * a.dtype.itemsize for a in args)
    touched += sum(a.size * a.dtype.itemsize for a in outs)
    specs = [pl.BlockSpec(memory_space=pltpu.HBM)] * apart
    specs += [pl.BlockSpec(memory_space=pltpu.VMEM)] * (len(args) - apart)
    return pl.pallas_call(
        body,
        out_shape=outs,
        in_specs=specs,
        out_specs=[pl.BlockSpec(memory_space=pltpu.HBM if far else pltpu.VMEM)] * len(outs),
        scratch_shapes=list(scratch),
        cost_estimate=pl.CostEstimate(
            flops=flops, bytes_accessed=touched, transcendentals=0
        ),
        compiler_params=pltpu.CompilerParams(vmem_limit_bytes=VMEM_BYTES),
    )(*args)


def shape(*dims, dtype=F32):
    return jax.ShapeDtypeStruct(dims, dtype)


def packed_rows(order):
    return order + (order - LANES) // 2


def pack_block(block, out):
    order = block.shape[0]
    tail = order - LANES
    out[0:order, :] = block[:, 0:LANES]
    corner = block[LANES:, LANES:]
    out[order : order + tail // 2, :] = jnp.concatenate(
        [corner[: tail // 2], corner[tail // 2 :]], axis=1
    )


def add_packed(block, packed, out):
    order = block.shape[0]
    tail = order - LANES
    out[:, 0:LANES] = block[:, 0:LANES] + packed[0:order, :]
    out[0:LANES, LANES:] = block[0:LANES, LANES:] + packed[LANES:order, :].T
    corner = packed[order : order + tail // 2, :]
    out[LANES:, LANES:] = block[LANES:, LANES:] + jnp.concatenate(
        [corner[:, :tail], corner[:, tail:]], axis=0
    )


def transposed(left, right):
    return lax.dot_general(
        left, right, (((0,), (0,)), ((), ())), preferred_element_type=F32
    )


def transposed(left, right):
    return lax.dot_general(
        left, right, (((0,), (0,)), ((), ())), preferred_element_type=F32
    )


def pack_body(face, kind, blocks, loads, functionals, out, field, block, ends, sems):
    base = packed_rows(block.shape[0])
    count = functionals.shape[1]
    copies = [
        pltpu.make_async_copy(blocks.at[face], block, sems.at[0]),
        pltpu.make_async_copy(loads.at[face], field, sems.at[1]),
        pltpu.make_async_copy(functionals.at[kind], ends, sems.at[2]),
    ]
    for copy in copies:
        copy.start()
    copies[0].wait()
    pack_block(block, out)
    copies[1].wait()
    copies[2].wait()
    part = product(halves(ends[...]), halves(field[...]))
    for step in range(part.shape[1] // LANES):
        out[base + step * count : base + (step + 1) * count, :] = part[
            :, step * LANES : (step + 1) * LANES
        ]


def own_body(order, wide_in, narrow_in, loads, functionals, out):
    base = packed_rows(order)
    count = functionals.shape[1]
    for kind, value in enumerate((loads[1], loads[3], loads[4] + loads[5])):
        out[kind * count : (kind + 1) * count, :] = product(
            halves(functionals[kind]), halves(value)
        )
    for kind, packed in ((0, wide_in), (1, narrow_in)):
        rows = slice(kind * count, (kind + 1) * count)
        for step in range(loads.shape[2] // LANES):
            lanes = slice(step * LANES, (step + 1) * LANES)
            part = packed[base + step * count : base + (step + 1) * count, :]
            out[rows, lanes] = out[rows, lanes] + part


def pair_body(own, other, out):
    rows = own.shape[0]
    member = lax.rem(lax.axis_index("wide"), 2)
    out[pl.ds(pl.multiple_of(member * rows, 8), rows), :] = own[...]
    out[pl.ds(pl.multiple_of((1 - member) * rows, 8), rows), :] = other[...]


def inverse_body(blocks, wide_in, narrow_in, high_out, low_out, sums, image, approx):
    add_packed(blocks[1], wide_in, sums.at[0])
    add_packed(blocks[3], narrow_in, sums.at[1])
    sums[2] = blocks[4] + blocks[5]
    for face in range(3):
        matrix = sums[face]
        largest = jnp.max(
            jnp.sum(jnp.abs(matrix), axis=1, keepdims=True), axis=0, keepdims=True
        )
        start = matrix / (largest * largest)
        approx[face] = start
        image[face] = product(halves(matrix), halves(start))
    for step in range(NS_STEPS):
        for face in range(3):
            current = image[face]
            left = halves(current)
            before = approx[face]
            after = 2.0 * before - product(left, halves(before))
            if step < NS_STEPS - 1:
                image[face] = 2.0 * current - product(left, left)
                approx[face] = after
            else:
                high_out[face], low_out[face] = halves(after)


def scaled_body(loads, wide_in, narrow_in, high, low, wide_out, narrow_out, own_out):
    for face, value, out in (
        (0, loads[1] + wide_in[...], wide_out),
        (1, loads[3] + narrow_in[...], narrow_out),
        (2, loads[4] + loads[5], own_out),
    ):
        out[...] = product((high[face], low[face]), halves(value))


def outgoing_body(
    blocks, solver, wide_below, wide_own, narrow_below, narrow_own, vertical,
    loads_out, wide_out,
):
    order = blocks.shape[1]
    for face, value in enumerate(
        (wide_below, wide_own, narrow_below, narrow_own, vertical, vertical)
    ):
        loads_out[face * order : (face + 1) * order, :] = product(
            halves(blocks[face]), halves(value[...])
        ).astype(BF16)
    solved = mxu(solver[:order, :], loads_out[...])
    wide_out[...] = product(halves(blocks[0]), halves(solved))


def narrow_body(blocks, solver, loads, out):
    order = blocks.shape[1]
    solved = mxu(solver[2 * order : 3 * order, :], loads[...])
    out[...] = product(halves(blocks[2]), halves(solved))


def kept_body(blocks, solver, high, low, loads, out, solved):
    order = blocks.shape[1]
    solved[0:order] = mxu(solver[order : 2 * order, :], loads[...])
    solved[order:] = mxu(solver[3 * order :, :], loads[...])

    def weighted(face, spot):
        return product(
            halves(blocks[face]), halves(solved[spot * order : (spot + 1) * order])
        )

    for face, value in (
        (0, weighted(1, 0)), (1, weighted(3, 1)), (2, weighted(4, 2) + weighted(5, 3))
    ):
        out[face] = product((high[face], low[face]), halves(value))


def returned_body(kept, high, low, wide_in, narrow_in, wide_out, narrow_out):
    for face, value, out in ((0, wide_in, wide_out), (1, narrow_in, narrow_out)):
        out[...] = kept[face] + product((high[face], low[face]), halves(value[...]))


def ring_group(place, groups):
    place = place % groups
    if place == 0:
        return 0
    return 2 * place - 1 if place <= groups // 2 else 2 * (groups - place)


def ring_place(group, groups):
    return next(p for p in range(groups) if ring_group(p, groups) == group)


def ring_origin(groups, step):
    group = lax.div(lax.axis_index("wide"), lax.axis_size("wide") // groups)
    origin = jnp.int32(0)
    for own in range(groups):
        other = ring_group(ring_place(own, groups) + step, groups)
        origin = jnp.where(group == own, other, origin)
    return origin


def lent_body(groups, matrix, out):
    width = out.shape[1]
    origin = ring_origin(groups, groups // 2)
    for group in range(groups):

        @pl.when(origin == group)
        def _():
            out[...] = matrix[:, group * width : (group + 1) * width]


def far_body(held, pair, kept, sent, total):
    total[...] = product(halves(held[...]), halves(pair[...]))
    across, members = lax.axis_index("narrow"), lax.axis_size("narrow")
    share = total.shape[0] // members
    for out, first in ((kept, 0), (sent, 1)):
        for place, step in enumerate(range(first, members, 2)):
            spot = pl.multiple_of((across ^ step) * share, 8)
            out[place * share : (place + 1) * share] = total[pl.ds(spot, share), :]


def fold_body(share, kept_in, received, kept, sent):
    for place in range(kept_in.shape[0] // share):
        span = slice(place * share, (place + 1) * share)
        out = (kept, sent)[place % 2]
        spot = place // 2 * share
        out[spot : spot + share] = kept_in[span] + received[span]


def sum_body(kept_in, received, out):
    out[...] = kept_in[...] + received[...]


def coarse_body(groups, matrix, *rest):
    steps = [step for step in range(1, groups) if 2 * step != groups]
    copies, (*outs, gathered) = rest[: 1 + 2 * len(steps)], rest[1 + 2 * len(steps) :]
    length = copies[0].shape[0]
    member = lax.rem(lax.axis_index("wide"), 2)

    def rows(step):
        spot = ring_origin(groups, step) * length
        return pl.ds(pl.multiple_of(spot, 8), length)

    gathered[rows(0), :] = copies[0][...]
    gathered[rows(groups // 2), :] = jnp.zeros_like(copies[0])
    for place, step in enumerate(steps):
        even, odd = copies[1 + 2 * place : 3 + 2 * place]
        gathered[rows(step), :] = jnp.where(member == 0, even[...], odd[...])
    total = product(halves(matrix[...]), halves(gathered[0 : matrix.shape[1]]))
    gathered[0 : total.shape[0], :] = total
    across, members = lax.axis_index("narrow"), len(outs)
    share = outs[0].shape[0]
    for step in range(members):
        spot = pl.multiple_of(lax.rem(across + step, members) * share, 8)
        outs[step][...] = gathered[pl.ds(spot, share), :]


def final_body(kept, wide_part, narrow_part, functionals, *rest):
    (*parts, out, held, sems) = rest
    count = functionals.shape[1]
    coarse = parts[0][...]
    for part in parts[1:]:
        coarse = coarse + part[...]
    copies = []
    for face, local in enumerate((wide_part[...], narrow_part[...], kept[2])):
        rows_high, rows_low = halves(coarse[face * count : (face + 1) * count])
        ends_high, ends_low = halves(functionals[face])
        held[face] = local + (
            transposed(ends_high, rows_high)
            + (transposed(ends_high, rows_low) + transposed(ends_low, rows_high))
        )
        copies.append(pltpu.make_async_copy(held.at[face], out.at[face], sems.at[face]))
        copies[-1].start()
    for copy in copies:
        copy.wait()


def along(value, axis, target):
    pairs = [(source, target(source)) for source in range(lax.axis_size(axis))]
    return lax.ppermute(value, axis, pairs)


def shifted(value, axis, steps):
    count = lax.axis_size(axis)
    return along(value, axis, lambda source: (source + steps) % count)


def apply(residual, face_schur, local_solver, functionals, coarse_inverse):
    blocks, loads, solver = face_schur[0, 0], residual[0, 0], local_solver[0, 0]
    functionals = jnp.swapaxes(functionals, 1, 2)
    order, columns = loads.shape[1:]
    count = functionals.shape[1]
    wide, narrow = lax.axis_size("wide"), lax.axis_size("narrow")
    field = shape(order, columns)
    field_flops = 6 * order * order * columns

    packed = shape(packed_rows(order) + count * columns // LANES, LANES)

    def pack(face, kind):
        return call(
            functools.partial(pack_body, face, kind),
            [packed, field],
            [
                pltpu.with_memory_space_constraint(blocks, pltpu.HBM),
                pltpu.with_memory_space_constraint(loads, pltpu.HBM),
                pltpu.with_memory_space_constraint(functionals, pltpu.HBM),
            ],
            flops=6 * order * columns * count,
            scratch=[
                pltpu.VMEM((order, order), F32),
                pltpu.VMEM((count, order), F32),
                pltpu.SemaphoreType.DMA((3,)),
            ],
            apart=3,
        )

    wide_low, wide_first = pack(0, 0)
    narrow_low, narrow_first = pack(2, 1)
    wide_above = shifted(wide_low, "wide", -1)
    narrow_above = shifted(narrow_low, "narrow", -1)
    wide_loads = shifted(wide_first, "wide", -1)
    narrow_loads = shifted(narrow_first, "narrow", -1)
    (own,) = call(
        functools.partial(own_body, order),
        [shape(3 * count, columns)],
        [wide_above, narrow_above, loads, functionals],
        flops=3 * 6 * order * columns * count,
    )
    halved = shape(3, order, order, dtype=BF16)
    high, low = call(
        inverse_body,
        [halved, halved],
        [blocks, wide_above, narrow_above],
        flops=3 * 24 * 6 * order**3,
        scratch=[pltpu.VMEM((3, order, order), F32)] * 3,
    )

    groups = wide // 2
    assert wide % 4 == 0 and narrow & (narrow - 1) == 0 and narrow > 1
    other = along(own, "wide", lambda i: i ^ 1)
    (pair,) = call(pair_body, [shape(6 * count, columns)], [own, other])

    def round_ring(value, steps, members):
        def target(i):
            if i % 2 not in members:
                return i
            place = ring_place(i // 2, groups) + steps
            return 2 * ring_group(place, groups) + i % 2

        return along(value, "wide", target)

    chunks = {}
    for member in range(2):
        rising = falling = pair
        for step in range(1, groups // 2):
            rising = round_ring(rising, 1, (member,))
            falling = round_ring(falling, -1, (member,))
            chunks[groups - step, member] = rising
            chunks[step, member] = falling
    rows = coarse_inverse.shape[0]
    share = shape(rows // narrow, columns)
    (lent,) = call(
        functools.partial(lent_body, groups),
        [shape(rows, pair.shape[0])],
        [coarse_inverse],
    )
    held = round_ring(lent, groups // 2, (0, 1))
    staying, going = call(
        far_body,
        [shape(rows // 2, columns)] * 2,
        [held, pair],
        flops=6 * held.size * columns,
        scratch=[pltpu.VMEM((rows, columns), F32)],
    )
    step = 1
    while 2 * step < narrow:
        received = along(going, "narrow", lambda j: j ^ step)
        step = 2 * step
        staying, going = call(
            functools.partial(fold_body, rows // narrow),
            [shape(rows // (2 * step), columns)] * 2,
            [staying, received],
        )
    received = along(going, "narrow", lambda j: j ^ step)
    (gone,) = call(sum_body, [share], [staying, received])
    home_coarse = round_ring(gone, groups // 2, (0, 1))
    shares = call(
        functools.partial(coarse_body, groups),
        [share] * narrow,
        [coarse_inverse, pair] + [chunks[key] for key in sorted(chunks)],
        flops=6 * coarse_inverse.size * columns,
        scratch=[pltpu.VMEM((max(coarse_inverse.shape), columns), F32)],
    )
    parts = [home_coarse, shares[0]] + [
        shifted(shares[step], "narrow", step) for step in range(1, narrow)
    ]

    wide_scaled, narrow_scaled, vertical = call(
        scaled_body,
        [field] * 3,
        [loads, wide_loads, narrow_loads, high, low],
        flops=3 * field_flops,
    )
    wide_below = shifted(wide_scaled, "wide", 1)
    narrow_below = shifted(narrow_scaled, "narrow", 1)
    local_loads, wide_back = call(
        outgoing_body,
        [shape(6 * order, columns, dtype=BF16), field],
        [blocks, solver, wide_below, wide_scaled, narrow_below, narrow_scaled, vertical],
        flops=7 * field_flops + 2 * 6 * order * order * columns,
    )
    (narrow_back,) = call(
        narrow_body,
        [field],
        [blocks, solver, local_loads],
        flops=field_flops + 2 * 6 * order * order * columns,
    )
    wide_returned = shifted(wide_back, "wide", -1)
    narrow_returned = shifted(narrow_back, "narrow", -1)
    (kept,) = call(
        kept_body,
        [shape(3, order, columns)],
        [blocks, solver, high, low, local_loads],
        flops=7 * field_flops + 4 * 2 * 6 * order * order * columns,
        scratch=[pltpu.VMEM((4 * order, columns), F32)],
    )
    wide_part, narrow_part = call(
        returned_body,
        [field, field],
        [kept, high, low, wide_returned, narrow_returned],
        flops=2 * field_flops,
    )
    (out,) = call(
        final_body,
        [shape(3, order, columns)],
        [kept, wide_part, narrow_part, functionals, *parts],
        flops=3 * 6 * order * count * columns,
        scratch=[pltpu.VMEM((3, order, columns), F32), pltpu.SemaphoreType.DMA((3,))],
        far=True,
    )
    return out[None, None]


def solution(mesh):
    placed = (
        P("wide", "narrow", None, None, None),
        P("wide", "narrow", None, None, None),
        P("wide", "narrow", None, None),
        P(),
        P("wide", "narrow"),
    )
    return jax.shard_map(
        apply,
        mesh=mesh,
        in_specs=placed,
        out_specs=P("wide", "narrow", None, None, None),
        check_vma=False,
    )
```

```python
import functools

import jax
import jax.numpy as jnp
from jax import lax
from jax.experimental import pallas as pl
from jax.experimental.pallas import tpu as pltpu
from jax.sharding import PartitionSpec as P

NS_STEPS = 12
LANES = 128
VMEM_BYTES = 24 * 2**20
F32 = jnp.float32
BF16 = jnp.bfloat16


def halves(value):
    high = value.astype(BF16)
    return high, (value - high.astype(F32)).astype(BF16)


def mxu(left, right):
    return jnp.dot(left, right, preferred_element_type=F32)


def product(left, right):
    left_high, left_low = left
    right_high, right_low = right
    return mxu(left_high, right_high) + (
        mxu(left_high, right_low) + mxu(left_low, right_high)
    )


def call(body, outs, args, flops=0, scratch=(), apart=0, far=False):
    touched = sum(a.size * a.dtype.itemsize for a in args)
    touched += sum(a.size * a.dtype.itemsize for a in outs)
    specs = [pl.BlockSpec(memory_space=pltpu.HBM)] * apart
    specs += [pl.BlockSpec(memory_space=pltpu.VMEM)] * (len(args) - apart)
    return pl.pallas_call(
        body,
        out_shape=outs,
        in_specs=specs,
        out_specs=[pl.BlockSpec(memory_space=pltpu.HBM if far else pltpu.VMEM)] * len(outs),
        scratch_shapes=list(scratch),
        cost_estimate=pl.CostEstimate(
            flops=flops, bytes_accessed=touched, transcendentals=0
        ),
        compiler_params=pltpu.CompilerParams(vmem_limit_bytes=VMEM_BYTES),
    )(*args)


def shape(*dims, dtype=F32):
    return jax.ShapeDtypeStruct(dims, dtype)


def packed_rows(order):
    return order + (order - LANES) // 2


def pack_block(block, out):
    order = block.shape[0]
    tail = order - LANES
    out[0:order, :] = block[:, 0:LANES]
    corner = block[LANES:, LANES:]
    out[order : order + tail // 2, :] = jnp.concatenate(
        [corner[: tail // 2], corner[tail // 2 :]], axis=1
    )


def add_packed(block, packed, out):
    order = block.shape[0]
    tail = order - LANES
    out[:, 0:LANES] = block[:, 0:LANES] + packed[0:order, :]
    out[0:LANES, LANES:] = block[0:LANES, LANES:] + packed[LANES:order, :].T
    corner = packed[order : order + tail // 2, :]
    out[LANES:, LANES:] = block[LANES:, LANES:] + jnp.concatenate(
        [corner[:, :tail], corner[:, tail:]], axis=0
    )


def transposed(left, right):
    return lax.dot_general(
        left, right, (((0,), (0,)), ((), ())), preferred_element_type=F32
    )


def transposed(left, right):
    return lax.dot_general(
        left, right, (((0,), (0,)), ((), ())), preferred_element_type=F32
    )


def pack_body(face, kind, blocks, loads, functionals, out, field, block, ends, sems):
    base = packed_rows(block.shape[0])
    count = functionals.shape[1]
    copies = [
        pltpu.make_async_copy(blocks.at[face], block, sems.at[0]),
        pltpu.make_async_copy(loads.at[face], field, sems.at[1]),
        pltpu.make_async_copy(functionals.at[kind], ends, sems.at[2]),
    ]
    for copy in copies:
        copy.start()
    copies[0].wait()
    pack_block(block, out)
    copies[1].wait()
    copies[2].wait()
    part = product(halves(ends[...]), halves(field[...]))
    for step in range(part.shape[1] // LANES):
        out[base + step * count : base + (step + 1) * count, :] = part[
            :, step * LANES : (step + 1) * LANES
        ]


def own_body(order, wide_in, narrow_in, loads, functionals, out):
    base = packed_rows(order)
    count = functionals.shape[1]
    for kind, value in enumerate((loads[1], loads[3], loads[4] + loads[5])):
        out[kind * count : (kind + 1) * count, :] = product(
            halves(functionals[kind]), halves(value)
        )
    for kind, packed in ((0, wide_in), (1, narrow_in)):
        rows = slice(kind * count, (kind + 1) * count)
        for step in range(loads.shape[2] // LANES):
            lanes = slice(step * LANES, (step + 1) * LANES)
            part = packed[base + step * count : base + (step + 1) * count, :]
            out[rows, lanes] = out[rows, lanes] + part


def pair_body(own, other, out):
    rows = own.shape[0]
    member = lax.rem(lax.axis_index("wide"), 2)
    out[pl.ds(pl.multiple_of(member * rows, 8), rows), :] = own[...]
    out[pl.ds(pl.multiple_of((1 - member) * rows, 8), rows), :] = other[...]


def inverse_body(blocks, wide_in, narrow_in, high_out, low_out, sums, image, approx):
    add_packed(blocks[1], wide_in, sums.at[0])
    add_packed(blocks[3], narrow_in, sums.at[1])
    sums[2] = blocks[4] + blocks[5]
    for face in range(3):
        matrix = sums[face]
        largest = jnp.max(
            jnp.sum(jnp.abs(matrix), axis=1, keepdims=True), axis=0, keepdims=True
        )
        start = matrix / (largest * largest)
        approx[face] = start
        image[face] = product(halves(matrix), halves(start))
    for step in range(NS_STEPS):
        for face in range(3):
            current = image[face]
            left = halves(current)
            before = approx[face]
            after = 2.0 * before - product(left, halves(before))
            if step < NS_STEPS - 1:
                image[face] = 2.0 * current - product(left, left)
                approx[face] = after
            else:
                high_out[face], low_out[face] = halves(after)


def scaled_body(loads, wide_in, narrow_in, high, low, wide_out, narrow_out, own_out):
    for face, value, out in (
        (0, loads[1] + wide_in[...], wide_out),
        (1, loads[3] + narrow_in[...], narrow_out),
        (2, loads[4] + loads[5], own_out),
    ):
        out[...] = product((high[face], low[face]), halves(value))


def outgoing_body(
    blocks, solver, wide_below, wide_own, narrow_below, narrow_own, vertical,
    loads_out, wide_out,
):
    order = blocks.shape[1]
    for face, value in enumerate(
        (wide_below, wide_own, narrow_below, narrow_own, vertical, vertical)
    ):
        loads_out[face * order : (face + 1) * order, :] = product(
            halves(blocks[face]), halves(value[...])
        ).astype(BF16)
    solved = mxu(solver[:order, :], loads_out[...])
    wide_out[...] = product(halves(blocks[0]), halves(solved))


def narrow_body(blocks, solver, loads, out):
    order = blocks.shape[1]
    solved = mxu(solver[2 * order : 3 * order, :], loads[...])
    out[...] = product(halves(blocks[2]), halves(solved))


def kept_body(blocks, solver, high, low, loads, out, solved):
    order = blocks.shape[1]
    solved[0:order] = mxu(solver[order : 2 * order, :], loads[...])
    solved[order:] = mxu(solver[3 * order :, :], loads[...])

    def weighted(face, spot):
        return product(
            halves(blocks[face]), halves(solved[spot * order : (spot + 1) * order])
        )

    for face, value in (
        (0, weighted(1, 0)), (1, weighted(3, 1)), (2, weighted(4, 2) + weighted(5, 3))
    ):
        out[face] = product((high[face], low[face]), halves(value))


def returned_body(kept, high, low, wide_in, narrow_in, wide_out, narrow_out):
    for face, value, out in ((0, wide_in, wide_out), (1, narrow_in, narrow_out)):
        out[...] = kept[face] + product((high[face], low[face]), halves(value[...]))


def ring_group(place, groups):
    place = place % groups
    if place == 0:
        return 0
    return 2 * place - 1 if place <= groups // 2 else 2 * (groups - place)


def ring_place(group, groups):
    return next(p for p in range(groups) if ring_group(p, groups) == group)


def ring_origin(groups, step):
    group = lax.div(lax.axis_index("wide"), lax.axis_size("wide") // groups)
    origin = jnp.int32(0)
    for own in range(groups):
        other = ring_group(ring_place(own, groups) + step, groups)
        origin = jnp.where(group == own, other, origin)
    return origin


def lent_body(groups, matrix, out):
    width = out.shape[1]
    origin = ring_origin(groups, groups // 2)
    for group in range(groups):

        @pl.when(origin == group)
        def _():
            out[...] = matrix[:, group * width : (group + 1) * width]


def far_body(held, pair, kept, sent, total):
    total[...] = product(halves(held[...]), halves(pair[...]))
    across, members = lax.axis_index("narrow"), lax.axis_size("narrow")
    share = total.shape[0] // members
    for out, first in ((kept, 0), (sent, 1)):
        for place, step in enumerate(range(first, members, 2)):
            spot = pl.multiple_of((across ^ step) * share, 8)
            out[place * share : (place + 1) * share] = total[pl.ds(spot, share), :]


def fold_body(share, kept_in, received, kept, sent):
    for place in range(kept_in.shape[0] // share):
        span = slice(place * share, (place + 1) * share)
        out = (kept, sent)[place % 2]
        spot = place // 2 * share
        out[spot : spot + share] = kept_in[span] + received[span]


def sum_body(kept_in, received, out):
    out[...] = kept_in[...] + received[...]


def coarse_body(groups, matrix, *rest):
    steps = [step for step in range(1, groups) if 2 * step != groups]
    copies, (*outs, gathered) = rest[: 1 + 2 * len(steps)], rest[1 + 2 * len(steps) :]
    length = copies[0].shape[0]
    member = lax.rem(lax.axis_index("wide"), 2)

    def rows(step):
        spot = ring_origin(groups, step) * length
        return pl.ds(pl.multiple_of(spot, 8), length)

    gathered[rows(0), :] = copies[0][...]
    gathered[rows(groups // 2), :] = jnp.zeros_like(copies[0])
    for place, step in enumerate(steps):
        even, odd = copies[1 + 2 * place : 3 + 2 * place]
        gathered[rows(step), :] = jnp.where(member == 0, even[...], odd[...])
    total = product(halves(matrix[...]), halves(gathered[0 : matrix.shape[1]]))
    gathered[0 : total.shape[0], :] = total
    across, members = lax.axis_index("narrow"), len(outs)
    share = outs[0].shape[0]
    for step in range(members):
        spot = pl.multiple_of(lax.rem(across + step, members) * share, 8)
        outs[step][...] = gathered[pl.ds(spot, share), :]


def final_body(kept, wide_part, narrow_part, functionals, *rest):
    (*parts, out, held, sems) = rest
    count = functionals.shape[1]
    coarse = parts[0][...]
    for part in parts[1:]:
        coarse = coarse + part[...]
    copies = []
    for face, local in enumerate((wide_part[...], narrow_part[...], kept[2])):
        rows_high, rows_low = halves(coarse[face * count : (face + 1) * count])
        ends_high, ends_low = halves(functionals[face])
        held[face] = local + (
            transposed(ends_high, rows_high)
            + (transposed(ends_high, rows_low) + transposed(ends_low, rows_high))
        )
        copies.append(pltpu.make_async_copy(held.at[face], out.at[face], sems.at[face]))
        copies[-1].start()
    for copy in copies:
        copy.wait()


def along(value, axis, target):
    pairs = [(source, target(source)) for source in range(lax.axis_size(axis))]
    return lax.ppermute(value, axis, pairs)


def shifted(value, axis, steps):
    count = lax.axis_size(axis)
    return along(value, axis, lambda source: (source + steps) % count)


def apply(residual, face_schur, local_solver, functionals, coarse_inverse):
    blocks, loads, solver = face_schur[0, 0], residual[0, 0], local_solver[0, 0]
    functionals = jnp.swapaxes(functionals, 1, 2)
    order, columns = loads.shape[1:]
    count = functionals.shape[1]
    wide, narrow = lax.axis_size("wide"), lax.axis_size("narrow")
    field = shape(order, columns)
    field_flops = 6 * order * order * columns

    packed = shape(packed_rows(order) + count * columns // LANES, LANES)

    def pack(face, kind):
        return call(
            functools.partial(pack_body, face, kind),
            [packed, field],
            [
                pltpu.with_memory_space_constraint(blocks, pltpu.HBM),
                pltpu.with_memory_space_constraint(loads, pltpu.HBM),
                pltpu.with_memory_space_constraint(functionals, pltpu.HBM),
            ],
            flops=6 * order * columns * count,
            scratch=[
                pltpu.VMEM((order, order), F32),
                pltpu.VMEM((count, order), F32),
                pltpu.SemaphoreType.DMA((3,)),
            ],
            apart=3,
        )

    wide_low, wide_first = pack(0, 0)
    narrow_low, narrow_first = pack(2, 1)
    wide_above = shifted(wide_low, "wide", -1)
    narrow_above = shifted(narrow_low, "narrow", -1)
    wide_loads = shifted(wide_first, "wide", -1)
    narrow_loads = shifted(narrow_first, "narrow", -1)
    (own,) = call(
        functools.partial(own_body, order),
        [shape(3 * count, columns)],
        [wide_above, narrow_above, loads, functionals],
        flops=3 * 6 * order * columns * count,
    )
    halved = shape(3, order, order, dtype=BF16)
    high, low = call(
        inverse_body,
        [halved, halved],
        [blocks, wide_above, narrow_above],
        flops=3 * 24 * 6 * order**3,
        scratch=[pltpu.VMEM((3, order, order), F32)] * 3,
    )

    groups = wide // 2
    assert wide % 4 == 0 and narrow & (narrow - 1) == 0 and narrow > 1
    other = along(own, "wide", lambda i: i ^ 1)
    (pair,) = call(pair_body, [shape(6 * count, columns)], [own, other])

    def round_ring(value, steps, members):
        def target(i):
            if i % 2 not in members:
                return i
            place = ring_place(i // 2, groups) + steps
            return 2 * ring_group(place, groups) + i % 2

        return along(value, "wide", target)

    chunks = {}
    rising, falling = [pair] * 2, [pair] * 2
    for step in range(1, groups // 2):
        rising = [round_ring(rising[0], 1, (0, 1))] * 2
        falling = [round_ring(falling[m], -1, (m,)) for m in range(2)]
        for member in range(2):
            chunks[groups - step, member] = rising[member]
            chunks[step, member] = falling[member]
    rows = coarse_inverse.shape[0]
    share = shape(rows // narrow, columns)
    (lent,) = call(
        functools.partial(lent_body, groups),
        [shape(rows, pair.shape[0])],
        [coarse_inverse],
    )
    held = round_ring(lent, groups // 2, (0, 1))
    staying, going = call(
        far_body,
        [shape(rows // 2, columns)] * 2,
        [held, pair],
        flops=6 * held.size * columns,
        scratch=[pltpu.VMEM((rows, columns), F32)],
    )
    step = 1
    while 2 * step < narrow:
        received = along(going, "narrow", lambda j: j ^ step)
        step = 2 * step
        staying, going = call(
            functools.partial(fold_body, rows // narrow),
            [shape(rows // (2 * step), columns)] * 2,
            [staying, received],
        )
    received = along(going, "narrow", lambda j: j ^ step)
    (gone,) = call(sum_body, [share], [staying, received])
    home_coarse = round_ring(gone, groups // 2, (0, 1))
    shares = call(
        functools.partial(coarse_body, groups),
        [share] * narrow,
        [coarse_inverse, pair] + [chunks[key] for key in sorted(chunks)],
        flops=6 * coarse_inverse.size * columns,
        scratch=[pltpu.VMEM((max(coarse_inverse.shape), columns), F32)],
    )
    parts = [home_coarse, shares[0]] + [
        shifted(shares[step], "narrow", step) for step in range(1, narrow)
    ]

    wide_scaled, narrow_scaled, vertical = call(
        scaled_body,
        [field] * 3,
        [loads, wide_loads, narrow_loads, high, low],
        flops=3 * field_flops,
    )
    wide_below = shifted(wide_scaled, "wide", 1)
    narrow_below = shifted(narrow_scaled, "narrow", 1)
    local_loads, wide_back = call(
        outgoing_body,
        [shape(6 * order, columns, dtype=BF16), field],
        [blocks, solver, wide_below, wide_scaled, narrow_below, narrow_scaled, vertical],
        flops=7 * field_flops + 2 * 6 * order * order * columns,
    )
    (narrow_back,) = call(
        narrow_body,
        [field],
        [blocks, solver, local_loads],
        flops=field_flops + 2 * 6 * order * order * columns,
    )
    wide_returned = shifted(wide_back, "wide", -1)
    narrow_returned = shifted(narrow_back, "narrow", -1)
    (kept,) = call(
        kept_body,
        [shape(3, order, columns)],
        [blocks, solver, high, low, local_loads],
        flops=7 * field_flops + 4 * 2 * 6 * order * order * columns,
        scratch=[pltpu.VMEM((4 * order, columns), F32)],
    )
    wide_part, narrow_part = call(
        returned_body,
        [field, field],
        [kept, high, low, wide_returned, narrow_returned],
        flops=2 * field_flops,
    )
    (out,) = call(
        final_body,
        [shape(3, order, columns)],
        [kept, wide_part, narrow_part, functionals, *parts],
        flops=3 * 6 * order * count * columns,
        scratch=[pltpu.VMEM((3, order, columns), F32), pltpu.SemaphoreType.DMA((3,))],
        far=True,
    )
    return out[None, None]


def solution(mesh):
    placed = (
        P("wide", "narrow", None, None, None),
        P("wide", "narrow", None, None, None),
        P("wide", "narrow", None, None),
        P(),
        P("wide", "narrow"),
    )
    return jax.shard_map(
        apply,
        mesh=mesh,
        in_specs=placed,
        out_specs=P("wide", "narrow", None, None, None),
        check_vma=False,
    )
```
